32 devices in a mesh: blk: 8 (over z, y), rhs: 4 (over x, core).
Axes of the slice: x: 2, y: 2, z: 4, core: 2. Of those that a mesh axis runs over, the one named last changes fastest.
Arguments:
- rhs: float32 [8, 8, 8, 256, 128], P(None, None, 'blk', 'rhs'), parts along dimension 3, may hold values from -6 to 6
- lower_tiles: bfloat16 [8, 8, 8, 3, 128, 128], P(None, None, 'blk'), may hold values from -0.25 to 0.25
- lower_block_columns: int32 [8, 8, 8, 3], P(None, None, 'blk'), may hold values from 0 to 511, as said below
- upper_tiles: bfloat16 [8, 8, 8, 3, 128, 128], P(None, None, 'blk'), may hold values from -0.25 to 0.25
- upper_cols: int32 [8, 8, 8, 3], P(None, None, 'blk'), may hold values from 0 to 511, as said below
- diag_inverse: bfloat16 [8, 8, 8, 128, 128], P(None, None, 'blk')
Outputs:
- solution: bfloat16 [8, 8, 8, 256, 128], P(None, None, 'blk', 'rhs'), parts along dimension 3
The draws below stay inside these ranges and needn't reach their ends.
There are 4 independent parts, one for each index of `rhs`. The reference program is written for one: setup_inputs(seed, part) draws one part's arguments, and reference() takes and returns one part's arrays. A program takes and returns all parts, laid end to end along the dimension named above; an argument that names none is the same for every part. Nothing has to cross between parts.
Inputs may be any that keep to these rules, and one draw needn't show every extreme that they name: `lower_block_columns`: entry k of block row (l * 8 + m) * 8 + p is either that row's own number (an empty slot) or ((l - 1) * 8 + m) * 8 + (p + d) mod 8 with d one of -1, 0, 1; the nonempty slots of a row have distinct d; rows with l = 0 have only empty slots. `upper_cols`: entry k of block row (l * 8 + m) * 8 + p is either that row's own number (an empty slot) or ((l + 1) * 8 + m) * 8 + (p + d) mod 8 with d one of -1, 0, 1; the nonempty slots of a row have distinct d; rows with l = 7 have only empty slots.
All inputs are finite; a program needn't handle non-finite values.
Results may differ from the reference program's by a relative error of at most 0.015.
Values may be sent and summed in bfloat16 or wider, within the bound.
A program may use at most 64 MiB of HBM per device.

```python
import math
import jax
import jax.numpy as jnp
from jax import lax

BLOCK = 128
SLOTS = 3
SIDES = 64
LEVELS = 8
ROW_DEV = 8
SPAN = 8


def pattern_columns(key, level_step, forced_row):
    dims_all = (LEVELS, ROW_DEV, SPAN, SLOTS)
    score_key, kept_key = jax.random.split(key)
    scores = jax.random.randint(score_key, dims_all, 0, 1 << 20) * 4 + lax.broadcasted_iota(jnp.int32, dims_all, 3)
    ranking = jnp.argsort(scores, axis=3, stable=True).astype(jnp.int32)
    offsets = ranking - 1
    levels = lax.broadcasted_iota(jnp.int32, dims_all, 0)
    places = lax.broadcasted_iota(jnp.int32, dims_all, 1)
    positions = lax.broadcasted_iota(jnp.int32, dims_all, 2)
    slot_ids = lax.broadcasted_iota(jnp.int32, dims_all, 3)
    numbers = (levels * ROW_DEV + places) * SPAN + positions
    target = ((levels + level_step) * ROW_DEV + places) * SPAN + (positions + offsets) % SPAN
    kept = jax.random.randint(kept_key, dims_all, 0, 4) > 0
    kept = kept & jnp.logical_not((numbers == forced_row) & (slot_ids == 0))
    inside = (levels + level_step >= 0) & (levels + level_step < LEVELS)
    return jnp.where(kept & inside, target, numbers).astype(jnp.int32)


def draw_lower_block_columns(key, part):
    return pattern_columns(jax.random.fold_in(key, 11), -1, LEVELS * ROW_DEV * SPAN - 1)


def draw_upper_cols(key, part):
    return pattern_columns(jax.random.fold_in(key, 23), 1, 0)


def draw_diag_inverse(key, part):
    dims_all = (LEVELS, ROW_DEV, SPAN, BLOCK, BLOCK)
    off_key, diagonal_key = jax.random.split(jax.random.fold_in(key, 37))
    off_part = jax.random.normal(off_key, dims_all, jnp.float32) * (0.6 / math.sqrt(BLOCK))
    diagonal_part = jax.random.uniform(diagonal_key, dims_all[:-1], jnp.float32, 0.7, 1.3)
    identity = (lax.broadcasted_iota(jnp.int32, (BLOCK, BLOCK), 0) == lax.broadcasted_iota(jnp.int32, (BLOCK, BLOCK), 1)).astype(jnp.float32)
    return (off_part * (1.0 - identity) + diagonal_part[..., None] * identity).astype(jnp.bfloat16)


def block_levels(stream_key, dims, cuts, least, largest):
    def one(axis_at, shards_of):
        draws = jax.random.uniform(jax.random.fold_in(jax.random.fold_in(stream_key, 6), axis_at), (shards_of,), jnp.float32, least / len(cuts), largest / len(cuts))
        return jnp.repeat(jnp.exp(draws), dims[axis_at] // shards_of).reshape((-1,) + (1,) * (len(dims) - axis_at - 1))

    level = one(*cuts[0])
    for cut in cuts[1:]:
        level = level * one(*cut)
    return level


def normal_values(stream_key, dims, spread, reach, pieces=(), kind=jnp.bfloat16):
    gain = block_levels(stream_key, dims, pieces, -0.22, 0.18) if pieces else 1.0
    result = jax.random.normal(stream_key, dims, jnp.float32) * spread * gain
    return jnp.minimum(jnp.maximum(result, -reach), reach).astype(kind)


def setup_inputs(seed: int = 0, part: int = 0) -> dict:
    streams_of = jax.random.split(jax.random.key(seed), 7)
    part_splits = jax.random.split(jax.random.fold_in(streams_of[6], part), 7)
    rhs = normal_values(part_splits[0], (LEVELS, ROW_DEV, SPAN, SIDES, BLOCK), 1.0, 6.0, ((2, 8),), jnp.float32)
    lower_tiles = normal_values(streams_of[1], (LEVELS, ROW_DEV, SPAN, SLOTS, BLOCK, BLOCK), (4 * BLOCK) ** -0.5, 0.25, ((2, 8),))
    lower_block_columns = draw_lower_block_columns(jax.random.fold_in(streams_of[6], 71), part)
    upper_tiles = normal_values(streams_of[3], (LEVELS, ROW_DEV, SPAN, SLOTS, BLOCK, BLOCK), (4 * BLOCK) ** -0.5, 0.25, ((2, 8),))
    upper_cols = draw_upper_cols(jax.random.fold_in(streams_of[6], 71), part)
    diag_inverse = draw_diag_inverse(jax.random.fold_in(streams_of[6], 71), part)
    return dict(rhs=rhs, lower_tiles=lower_tiles, lower_block_columns=lower_block_columns, upper_tiles=upper_tiles, upper_cols=upper_cols, diag_inverse=diag_inverse)


def level_products(solved, tile_collection, columns, numbers):
    chosen_entries = solved[columns].astype(jnp.float32)
    present = (columns != numbers[:, None]).astype(jnp.float32)
    chosen_entries = chosen_entries * present[:, :, None, None]
    return jnp.einsum("rksb,rkab->rsa", chosen_entries, tile_collection.astype(jnp.float32))


def reference(rhs, lower_tiles, lower_block_columns, upper_tiles, upper_cols, diag_inverse):
    per_level = ROW_DEV * SPAN
    row_total = LEVELS * per_level
    side_rows = rhs.reshape(LEVELS, per_level, SIDES, BLOCK)
    lower_tile_group = lower_tiles.reshape(LEVELS, per_level, SLOTS, BLOCK, BLOCK)
    lower_index = lower_block_columns.reshape(LEVELS, per_level, SLOTS)
    upper_set = upper_tiles.reshape(LEVELS, per_level, SLOTS, BLOCK, BLOCK)
    upper_index = upper_cols.reshape(LEVELS, per_level, SLOTS)
    inverse = diag_inverse.reshape(LEVELS, per_level, BLOCK, BLOCK)
    numbers_all = jnp.arange(row_total, dtype=jnp.int32).reshape(LEVELS, per_level)

    def forward(level_id, solved):
        numbers = numbers_all[level_id]
        products = level_products(solved, lower_tile_group[level_id], lower_index[level_id], numbers)
        solved_now = lax.optimization_barrier((side_rows[level_id] - products).astype(jnp.bfloat16))
        offset_row = (level_id * per_level).astype(jnp.int32)
        return lax.dynamic_update_slice_in_dim(solved, solved_now, offset_row, 0)

    forward_rows = lax.fori_loop(0, LEVELS, forward, jnp.zeros((row_total, SIDES, BLOCK), jnp.bfloat16))

    def backward(countdown, finished):
        level_id = LEVELS - 1 - countdown
        numbers = numbers_all[level_id]
        products = level_products(finished, upper_set[level_id], upper_index[level_id], numbers)
        offset_row = (level_id * per_level).astype(jnp.int32)
        current = lax.dynamic_slice_in_dim(forward_rows, offset_row, per_level, 0).astype(jnp.float32)
        summed_terms = lax.optimization_barrier((current - products).astype(jnp.bfloat16))
        solved_now = jnp.einsum("rsb,rab->rsa", summed_terms.astype(jnp.float32), inverse[level_id].astype(jnp.float32)).astype(jnp.bfloat16)
        return lax.dynamic_update_slice_in_dim(finished, lax.optimization_barrier(solved_now), offset_row, 0)

    finished = lax.fori_loop(0, LEVELS, backward, jnp.zeros((row_total, SIDES, BLOCK), jnp.bfloat16))
    return finished.reshape(LEVELS, ROW_DEV, SPAN, SIDES, BLOCK)
```

```python
import functools

import jax
import jax.numpy as jnp
from jax import lax
from jax.experimental import pallas as pl
from jax.experimental.pallas import tpu as pltpu
from jax.sharding import PartitionSpec as P

MESH = pl.DeviceIdType.MESH
VMEM_LIMIT = 52 * 2**20
AHEAD = 4


def product(x, tile):
    return lax.dot_general(x, tile, (((1,), (1,)), ((), ())), preferred_element_type=jnp.float32)


def sweep_kernel(
    n,
    parts,
    lower_cols,
    upper_cols,
    rhs,
    lower,
    upper,
    inverse,
    out,
    cols,
    rhs_v,
    rhs_b,
    lower_v,
    upper_v,
    inverse_v,
    chosen,
    acc,
    y,
    x,
    halo,
    rhs_sem,
    load_sem,
    cols_sem,
    tile_send,
    tile_recv,
    cols_send,
    cols_recv,
    side_send,
    side_recv,
    edge_send,
    row_send,
    row_recv,
    out_send,
    out_recv,
):
    levels, rows, sides, block = rhs.shape
    slots = lower.shape[2]
    owners = 2 * parts
    share = rows // owners
    last = levels - 1
    me = lax.axis_index("blk")
    part = lax.axis_index("rhs")
    half = lax.rem(me, 2)
    pair = me - half
    partner = pair + 1 - half
    owner = half * parts + part
    mine = owner * share
    others = range(1, owners)

    def other(k):
        return lax.rem(owner + k, owners)

    def device(first, s):
        return {"blk": first + s // parts, "rhs": lax.rem(s, parts)}

    def load_rhs(level):
        return pltpu.make_async_copy(rhs.at[level], rhs_v.at[level], rhs_sem.at[level])

    def load(kind, level):
        source, target = ((lower, lower_v), (upper, upper_v), (inverse, inverse_v))[kind]
        return pltpu.make_async_copy(
            source.at[level, pl.ds(mine, share)], target.at[level, half], load_sem.at[kind, level]
        )

    def load_cols(kind):
        return pltpu.make_async_copy((lower_cols, upper_cols)[kind], cols.at[kind, half], cols_sem.at[kind])

    def give_cols(kind):
        return pltpu.make_async_remote_copy(
            src_ref=(lower_cols, upper_cols)[kind],
            dst_ref=cols.at[kind, half],
            send_sem=cols_send.at[kind],
            recv_sem=cols_recv.at[kind],
            device_id={"blk": partner},
            device_id_type=MESH,
        )

    def give_tiles(kind, level):
        source, target = ((lower, lower_v), (upper, upper_v), (inverse, inverse_v))[kind]
        theirs = ((1 - half) * parts + part) * share
        return pltpu.make_async_remote_copy(
            src_ref=source.at[level, pl.ds(theirs, share)],
            dst_ref=target.at[level, half],
            send_sem=tile_send.at[kind, level],
            recv_sem=tile_recv.at[kind, level],
            device_id={"blk": partner},
            device_id_type=MESH,
        )

    def give_sides(level, k):
        s = other(k)
        return pltpu.make_async_remote_copy(
            src_ref=rhs_b.at[level, pl.ds(s * share, share)],
            dst_ref=y.at[level, :, owner],
            send_sem=side_send.at[level, s],
            recv_sem=side_recv.at[level, owner],
            device_id=device(pair, s),
            device_id_type=MESH,
        )

    def take_sides(level, k):
        s = other(k)
        pltpu.make_async_remote_copy(
            src_ref=rhs_b.at[level, pl.ds(s * share, share)],
            dst_ref=y.at[level, :, s],
            send_sem=side_send.at[level, s],
            recv_sem=side_recv.at[level, s],
            device_id=device(pair, s),
            device_id_type=MESH,
        ).wait_recv()

    def give_edge(s, i):
        beside = lax.rem(pair + 4 * half - 2 + n, n)
        return pltpu.make_async_remote_copy(
            src_ref=rhs_b.at[0, s * share + i],
            dst_ref=halo.at[0, 0, i, part, half],
            send_sem=edge_send.at[s, i],
            recv_sem=row_recv.at[0, 0, i, part, half],
            device_id=device(beside, s),
            device_id_type=MESH,
        )

    def give_row(own, sweep, level, i, j, way):
        return pltpu.make_async_remote_copy(
            src_ref=own.at[level, i, way * parts + j],
            dst_ref=halo.at[sweep, level, i, j, way],
            send_sem=row_send.at[sweep, level, i, j, way],
            recv_sem=row_recv.at[sweep, level, i, j, way],
            device_id={"blk": lax.rem(me + 4 * way - 2 + n, n)},
            device_id_type=MESH,
        )

    def give_out(level, k):
        s = other(k)
        return pltpu.make_async_remote_copy(
            src_ref=x.at[level, :, s],
            dst_ref=out.at[level, pl.ds(mine, share)],
            send_sem=out_send.at[level, s],
            recv_sem=out_recv.at[level, owner],
            device_id=device(pair, s),
            device_id_type=MESH,
        )

    def keep_out(level):
        return pltpu.make_async_copy(
            x.at[level, :, owner], out.at[level, pl.ds(mine, share)], out_send.at[level, owner]
        )

    def take_out(level, k):
        s = other(k)
        pltpu.make_async_remote_copy(
            src_ref=x.at[level, :, s],
            dst_ref=out.at[level, pl.ds(s * share, share)],
            send_sem=out_send.at[level, s],
            recv_sem=out_recv.at[level, s],
            device_id=device(pair, s),
            device_id_type=MESH,
        ).wait_recv()

    def each(first, end, action):
        def step(level, carry):
            action(level)
            return carry

        lax.fori_loop(first, end, step, 0)

    load_rhs(0).start()
    barrier = pltpu.get_barrier_semaphore()

    def greet(first, s):
        pl.semaphore_signal(barrier, inc=1, device_id=device(first, s), device_id_type=MESH)

    for s in range(owners):
        greet(lax.rem(pair + 4 * half - 2 + n, n), s)
    for s in range(parts):
        greet(lax.rem(pair + 2 - 4 * half + n, n), half * parts + s)
    for k in others:
        greet(pair, other(k))
    each(1, levels, lambda level: load_rhs(level).start())
    load_cols(0).start()
    load_cols(1).start()
    each(1, levels, lambda level: load(0, level).start())
    each(0, levels, lambda level: load(2, last - level).start())
    each(1, levels, lambda level: load(1, last - level).start())

    def narrow(level):
        load_rhs(level).wait()
        rhs_b[level] = rhs_v[level].astype(jnp.bfloat16)
        for i in range(share):
            y[level, i, owner] = rhs_v[level, mine + i].astype(jnp.bfloat16)

    each(0, levels, narrow)
    pl.semaphore_wait(barrier, 2 * owners + parts - 1)

    def forward_item(level):
        for k in others:
            give_sides(level, k).start()
        give_tiles(0, level).start()

    def backward_item(level):
        @pl.when(level < last)
        def _():
            give_tiles(1, level).start()

        give_tiles(2, level).start()

    def ahead_forward(level):
        @pl.when(level + AHEAD <= last)
        def _():
            forward_item(level + AHEAD)

        @pl.when(level + AHEAD > last)
        def _():
            backward_item(2 * last + 1 - AHEAD - level)

    def ahead_backward(turn):
        @pl.when(turn + AHEAD - 1 <= last)
        def _():
            backward_item(last - turn - AHEAD + 1)

    for s in range(owners):
        for i in range(share):
            give_edge(s, i).start()
    for k in others:
        give_sides(0, k).start()
    give_cols(0).start()
    give_cols(1).start()
    each(1, AHEAD + 1, forward_item)
    for k in others:
        take_sides(0, k)
    for kind in range(2):
        load_cols(kind).wait()
        give_cols(kind).wait_recv()

    def choose(sweep, level, source, tiles):
        for i in range(share):
            base = (source * rows + mine + i) * n
            for p in range(2):
                for d in range(3):
                    wanted = base + lax.rem(pair + p + d - 1 + n, n)
                    tile = jnp.zeros((block, block), tiles.dtype)
                    for k in range(slots):
                        found = cols[sweep, p, level, k, 0, mine + i] == wanted
                        tile = lax.select(found, tiles[level, p, i, k], tile)
                    chosen[i, p, d] = tile

    def early(sweep, level, source, own):
        for i in range(share):
            first = own[source, i, 0:parts].reshape(parts * sides, block)
            second = own[source, i, parts:owners].reshape(parts * sides, block)
            for p in range(2):
                start = y[level, i, p * parts : (p + 1) * parts].reshape(parts * sides, block)
                terms = product(first, chosen[i, p, 1 - p]) + product(second, chosen[i, p, 2 - p])
                acc[i, p] = (start.astype(jnp.float32) - terms).reshape(parts, sides, block)

    def late(own, sweep, source, i, j):
        for way in range(2):
            give_row(own, sweep, source, i, j, way).wait_recv()
        low = acc[i, 0, j] - product(halo[sweep, source, i, j, 1], chosen[i, 0, 0])
        high = acc[i, 1, j] - product(halo[sweep, source, i, j, 0], chosen[i, 1, 2])
        return low.astype(jnp.bfloat16), high.astype(jnp.bfloat16)

    def arrive_forward(level):
        for k in others:
            take_sides(level, k)
        load(0, level).wait()
        give_tiles(0, level).wait_recv()

    def forward(level):
        arrive_forward(level)
        choose(0, level, level - 1, lower_v)
        early(0, level, level - 1, y)
        for i in range(share):
            for j in range(parts):
                low, high = late(y, 0, level - 1, i, j)
                y[level, i, j] = low
                y[level, i, parts + j] = high
                for way in range(2):
                    give_row(y, 0, level, i, j, way).start()
        ahead_forward(level)

    each(1, last, forward)

    def solve(level, i, j, low, high):
        x[level, i, j] = product(low, inverse_v[level, 0, i]).astype(jnp.bfloat16)
        x[level, i, parts + j] = product(high, inverse_v[level, 1, i]).astype(jnp.bfloat16)

    def leave(level):
        for k in others:
            give_out(level, k).start()
        keep_out(level).start()

    arrive_forward(last)
    load(2, last).wait()
    give_tiles(2, last).wait_recv()
    choose(0, last, last - 1, lower_v)
    early(0, last, last - 1, y)
    for i in range(share):
        for j in range(parts):
            low, high = late(y, 0, last - 1, i, j)
            solve(last, i, j, low, high)
            for way in range(2):
                give_row(x, 1, last, i, j, way).start()
    ahead_forward(last)
    leave(last)

    def backward(turn):
        level = last - turn
        load(1, level).wait()
        give_tiles(1, level).wait_recv()
        load(2, level).wait()
        give_tiles(2, level).wait_recv()
        choose(1, level, level + 1, upper_v)
        early(1, level, level + 1, x)
        for i in range(share):
            for j in range(parts):
                low, high = late(x, 1, level + 1, i, j)
                solve(level, i, j, low, high)

                @pl.when(level > 0)
                def _():
                    for way in range(2):
                        give_row(x, 1, level, i, j, way).start()

        ahead_backward(turn)
        leave(level)

    each(1, levels, backward)

    for kind in range(2):
        give_cols(kind).wait_send()
    for s in range(owners):
        for i in range(share):
            give_edge(s, i).wait_send()

    def finish(level):
        for k in others:
            give_sides(level, k).wait_send()
            give_out(level, k).wait_send()
            take_out(level, k)
        keep_out(level).wait()
        give_tiles(2, level).wait_send()

    each(0, levels, finish)

    def finish_tiles(level):
        give_tiles(0, level).wait_send()
        give_tiles(1, level - 1).wait_send()
        for i in range(share):
            for j in range(parts):
                for way in range(2):
                    give_row(x, 1, level, i, j, way).wait_send()

    each(1, levels, finish_tiles)

    def finish_rows(level):
        for i in range(share):
            for j in range(parts):
                for way in range(2):
                    give_row(y, 0, level, i, j, way).wait_send()

    each(1, last, finish_rows)


def on_device(n, parts, rhs, lower_tiles, lower_block_columns, upper_tiles, upper_cols, diag_inverse):
    rhs = rhs[:, :, 0]
    lower = lower_tiles[:, :, 0]
    upper = upper_tiles[:, :, 0]
    inverse = diag_inverse[:, :, 0]
    levels, rows, sides, block = rhs.shape
    slots = lower.shape[2]
    owners = 2 * parts
    share = rows // owners
    half = jnp.bfloat16
    dma = pltpu.SemaphoreType.DMA
    any_space = pl.BlockSpec(memory_space=pl.ANY)
    tiles = pltpu.VMEM((levels, 2, share, slots, block, block), half)
    own = pltpu.VMEM((levels, share, owners, sides, block), half)
    result = pl.pallas_call(
        functools.partial(sweep_kernel, n, parts),
        out_shape=jax.ShapeDtypeStruct(rhs.shape, half),
        in_specs=[any_space] * 6,
        out_specs=any_space,
        scratch_shapes=[
            pltpu.SMEM((2, 2, levels, slots, 1, rows), jnp.int32),
            pltpu.VMEM(rhs.shape, rhs.dtype),
            pltpu.VMEM(rhs.shape, half),
            tiles,
            tiles,
            pltpu.VMEM((levels, 2, share, block, block), half),
            pltpu.VMEM((share, 2, 3, block, block), half),
            pltpu.VMEM((share, 2, parts, sides, block), jnp.float32),
            own,
            own,
            pltpu.VMEM((2, levels, share, parts, 2, sides, block), half),
            dma((levels,)),
            dma((3, levels)),
            dma((2,)),
            dma((3, levels)),
            dma((3, levels)),
            dma((2,)),
            dma((2,)),
            dma((levels, owners)),
            dma((levels, owners)),
            dma((owners, share)),
            dma((2, levels, share, parts, 2)),
            dma((2, levels, share, parts, 2)),
            dma((levels, owners)),
            dma((levels, owners)),
        ],
        compiler_params=pltpu.CompilerParams(collective_id=0, has_side_effects=True, vmem_limit_bytes=VMEM_LIMIT),
    )(
        lower_block_columns.transpose(0, 3, 2, 1),
        upper_cols.transpose(0, 3, 2, 1),
        rhs,
        lower,
        upper,
        inverse,
    )
    return result[:, :, None]


def solution(mesh):
    return jax.shard_map(
        functools.partial(on_device, mesh.shape["blk"], mesh.shape["rhs"]),
        mesh=mesh,
        in_specs=(
            P(None, None, "blk", "rhs", None),
            P(None, None, "blk", None, None, None),
            P(None, None, "blk", None),
            P(None, None, "blk", None, None, None),
            P(None, None, "blk", None),
            P(None, None, "blk", None, None),
        ),
        out_specs=P(None, None, "blk", "rhs", None),
        check_vma=False,
    )
```

```python
import functools

import jax
import jax.numpy as jnp
from jax import lax
from jax.experimental import pallas as pl
from jax.experimental.pallas import tpu as pltpu
from jax.sharding import PartitionSpec as P

MESH = pl.DeviceIdType.MESH
VMEM_LIMIT = 52 * 2**20
AHEAD = 4


def product(x, tile):
    return lax.dot_general(x, tile, (((1,), (1,)), ((), ())), preferred_element_type=jnp.float32)


def sweep_kernel(
    n,
    parts,
    lower_cols,
    upper_cols,
    rhs,
    lower,
    upper,
    inverse,
    out,
    cols,
    rhs_v,
    rhs_b,
    lower_v,
    upper_v,
    inverse_v,
    chosen,
    acc,
    y,
    x,
    halo,
    rhs_sem,
    load_sem,
    cols_sem,
    tile_send,
    tile_recv,
    side_send,
    side_recv,
    edge_send,
    row_send,
    row_recv,
    out_sem,
):
    levels, rows, sides, block = rhs.shape
    slots = lower.shape[2]
    owners = 2 * parts
    share = rows // owners
    last = levels - 1
    me = lax.axis_index("blk")
    part = lax.axis_index("rhs")
    half = lax.rem(me, 2)
    pair = me - half
    partner = pair + 1 - half
    owner = half * parts + part
    mine = owner * share
    others = range(1, owners)

    def other(k):
        return lax.rem(owner + k, owners)

    def device(first, s):
        return {"blk": first + s // parts, "rhs": lax.rem(s, parts)}

    def load_rhs(first, count):
        span = pl.ds(first, count)
        return pltpu.make_async_copy(rhs.at[span], rhs_v.at[span], rhs_sem.at[min(first, 1)])

    def tiles_of(kind):
        return ((lower, lower_v), (upper, upper_v), (inverse, inverse_v))[kind]

    spans = (pl.ds(1, last), pl.ds(0, last), pl.ds(0, levels))

    def load(kind):
        source, target = tiles_of(kind)
        span = spans[kind]
        return pltpu.make_async_copy(
            source.at[span, pl.ds(mine, share)], target.at[span, half], load_sem.at[kind]
        )

    def load_cols(kind):
        return pltpu.make_async_copy((lower_cols, upper_cols)[kind], cols.at[half, kind], cols_sem.at[0, kind])

    def remote(source, target, send_sem, recv_sem, device_id):
        return pltpu.make_async_remote_copy(
            src_ref=source,
            dst_ref=target,
            send_sem=send_sem,
            recv_sem=recv_sem,
            device_id=device_id,
            device_id_type=MESH,
        )

    def give_cols(kind):
        return remote(
            (lower_cols, upper_cols)[kind],
            cols.at[half, kind],
            cols_sem.at[1, kind],
            cols_sem.at[2, kind],
            {"blk": partner},
        )

    def give_tiles(kind, level):
        source, target = tiles_of(kind)
        theirs = ((1 - half) * parts + part) * share
        return remote(
            source.at[level, pl.ds(theirs, share)],
            target.at[level, half],
            tile_send.at[kind],
            tile_recv.at[kind, level],
            {"blk": partner},
        )

    def tiles_given(kind):
        source, target = tiles_of(kind)
        span = spans[kind]
        remote(
            source.at[span, pl.ds(0, share)], target.at[span, half], tile_send.at[kind], tile_recv.at[kind, 0], {"blk": partner}
        ).wait_send()

    def give_sides(level, k):
        s = other(k)
        return remote(
            rhs_b.at[level, pl.ds(s * share, share)],
            y.at[level, :, owner],
            side_send.at[0],
            side_recv.at[level],
            device(pair, s),
        )

    def sides_given():
        whole = rhs_b.at[:, pl.ds(0, rows - share)]
        remote(whole, whole, side_send.at[0], side_recv.at[0], {"blk": partner}).wait_send()

    def take_sides(level):
        whole = y.at[level, :, pl.ds(0, owners - 1)]
        remote(whole, whole, side_send.at[0], side_recv.at[level], {"blk": partner}).wait_recv()

    def give_edge(s, i):
        beside = lax.rem(pair + 4 * half - 2 + n, n)
        return remote(
            rhs_b.at[0, s * share + i],
            halo.at[0, 0, i, part, half],
            edge_send.at[0],
            row_recv.at[0, i, part],
            device(beside, s),
        )

    def edges_given():
        remote(rhs_b.at[0], rhs_b.at[0], edge_send.at[0], row_recv.at[0, 0, 0], {"blk": partner}).wait_send()

    def turn_of(sweep, level):
        return lax.rem(level if sweep == 0 else 2 * last - level, 2)

    def give_row(own, sweep, level, i, j, way):
        return remote(
            own.at[level, i, way * parts + j],
            halo.at[sweep, level, i, j, way],
            row_send.at[sweep],
            row_recv.at[turn_of(sweep, level), i, j],
            {"blk": lax.rem(me + 4 * way - 2 + n, n)},
        )

    def take_rows(sweep, level, i, j):
        whole = halo.at[sweep, level, i, j]
        remote(
            whole, whole, row_send.at[sweep], row_recv.at[turn_of(sweep, level), i, j], {"blk": partner}
        ).wait_recv()

    def rows_given(own, sweep, count):
        whole = own.at[pl.ds(1, count)]
        remote(whole, whole, row_send.at[sweep], row_recv.at[0, 0, 0], {"blk": partner}).wait_send()

    def give_out(level, k):
        s = other(k)
        return remote(
            x.at[level, :, s],
            out.at[level, pl.ds(mine, share)],
            out_sem.at[0],
            out_sem.at[1],
            device(pair, s),
        )

    def keep_out(level):
        return pltpu.make_async_copy(x.at[level, :, owner], out.at[level, pl.ds(mine, share)], out_sem.at[2])

    def outs_done():
        sent = x.at[:, :, pl.ds(0, owners - 1)]
        kept = x.at[:, :, owner]
        got = out.at[:, pl.ds(0, rows - share)]
        pltpu.make_async_copy(kept, out.at[:, pl.ds(mine, share)], out_sem.at[2]).wait()
        remote(sent, sent, out_sem.at[0], out_sem.at[1], {"blk": partner}).wait_send()
        remote(got, got, out_sem.at[0], out_sem.at[1], {"blk": partner}).wait_recv()

    def each(first, end, action):
        def step(level, carry):
            action(level)
            return carry

        lax.fori_loop(first, end, step, 0)

    load_rhs(0, 1).start()
    barrier = pltpu.get_barrier_semaphore()

    def greet(first, s):
        pl.semaphore_signal(barrier, inc=1, device_id=device(first, s), device_id_type=MESH)

    for s in range(owners):
        greet(lax.rem(pair + 4 * half - 2 + n, n), s)
    for s in range(parts):
        greet(lax.rem(pair + 2 - 4 * half + n, n), half * parts + s)
    for k in others:
        greet(pair, other(k))
    load_rhs(1, last).start()
    for kind in range(2):
        load_cols(kind).start()
    for kind in range(3):
        load(kind).start()

    def narrow(level):
        rhs_b[level] = rhs_v[level].astype(jnp.bfloat16)
        for i in range(share):
            y[level, i, owner] = rhs_v[level, mine + i].astype(jnp.bfloat16)

    load_rhs(0, 1).wait()
    narrow(0)
    pl.semaphore_wait(barrier, 2 * owners + parts - 1)
    for k in others:
        give_sides(0, k).start()
    for s in range(owners):
        for i in range(share):
            give_edge(s, i).start()
    give_cols(0).start()
    give_cols(1).start()

    def forward_item(level):
        for k in others:
            give_sides(level, k).start()
        give_tiles(0, level).start()

    def backward_item(level):
        @pl.when(level < last)
        def _():
            give_tiles(1, level).start()

        give_tiles(2, level).start()

    def ahead_forward(level):
        @pl.when(level + AHEAD <= last)
        def _():
            forward_item(level + AHEAD)

        @pl.when(level + AHEAD > last)
        def _():
            backward_item(2 * last + 1 - AHEAD - level)

    def ahead_backward(turn):
        @pl.when(turn + AHEAD - 1 <= last)
        def _():
            backward_item(last - turn - AHEAD + 1)

    def open_item(level):
        narrow(level)
        forward_item(level)

    load_rhs(1, last).wait()
    each(1, AHEAD + 1, open_item)
    each(AHEAD + 1, levels, narrow)
    take_sides(0)
    for kind in range(2):
        load_cols(kind).wait()
        give_cols(kind).wait_recv()
    for kind in range(3):
        load(kind).wait()

    def choose(sweep, level, source, tiles):
        for i in range(share):
            base = (source * rows + mine + i) * n
            for p in range(2):
                for d in range(3):
                    wanted = base + lax.rem(pair + p + d - 1 + n, n)
                    tile = jnp.zeros((block, block), tiles.dtype)
                    for k in range(slots):
                        found = cols[p, sweep, level, k, 0, mine + i] == wanted
                        tile = lax.select(found, tiles[level, p, i, k], tile)
                    chosen[i, p, d] = tile

    def early(sweep, level, source, own):
        for i in range(share):
            first = own[source, i, 0:parts].reshape(parts * sides, block)
            second = own[source, i, parts:owners].reshape(parts * sides, block)
            for p in range(2):
                start = y[level, i, p * parts : (p + 1) * parts].reshape(parts * sides, block)
                terms = product(first, chosen[i, p, 1 - p]) + product(second, chosen[i, p, 2 - p])
                acc[i, p] = (start.astype(jnp.float32) - terms).reshape(parts, sides, block)

    def late(own, sweep, source, i, j):
        take_rows(sweep, source, i, j)
        low = acc[i, 0, j] - product(halo[sweep, source, i, j, 1], chosen[i, 0, 0])
        high = acc[i, 1, j] - product(halo[sweep, source, i, j, 0], chosen[i, 1, 2])
        return low.astype(jnp.bfloat16), high.astype(jnp.bfloat16)

    def arrive_forward(level):
        take_sides(level)
        give_tiles(0, level).wait_recv()

    def forward(level):
        arrive_forward(level)
        choose(0, level, level - 1, lower_v)
        early(0, level, level - 1, y)
        for i in range(share):
            for j in range(parts):
                low, high = late(y, 0, level - 1, i, j)
                y[level, i, j] = low
                y[level, i, parts + j] = high
                for way in range(2):
                    give_row(y, 0, level, i, j, way).start()
        ahead_forward(level)

    each(1, last, forward)

    def solve(level, i, j, low, high):
        x[level, i, j] = product(low, inverse_v[level, 0, i]).astype(jnp.bfloat16)
        x[level, i, parts + j] = product(high, inverse_v[level, 1, i]).astype(jnp.bfloat16)

    def leave(level):
        for k in others:
            give_out(level, k).start()
        keep_out(level).start()

    arrive_forward(last)
    give_tiles(2, last).wait_recv()
    choose(0, last, last - 1, lower_v)
    early(0, last, last - 1, y)
    for i in range(share):
        for j in range(parts):
            low, high = late(y, 0, last - 1, i, j)
            solve(last, i, j, low, high)
            for way in range(2):
                give_row(x, 1, last, i, j, way).start()
    ahead_forward(last)
    leave(last)

    def backward(turn):
        level = last - turn
        give_tiles(1, level).wait_recv()
        give_tiles(2, level).wait_recv()
        choose(1, level, level + 1, upper_v)
        early(1, level, level + 1, x)
        for i in range(share):
            for j in range(parts):
                low, high = late(x, 1, level + 1, i, j)
                solve(level, i, j, low, high)

                @pl.when(level > 0)
                def _():
                    for way in range(2):
                        give_row(x, 1, level, i, j, way).start()

        ahead_backward(turn)
        leave(level)

    each(1, levels, backward)

    for kind in range(2):
        give_cols(kind).wait_send()
    edges_given()
    sides_given()
    rows_given(y, 0, last - 1)
    rows_given(x, 1, last)
    for kind in range(3):
        tiles_given(kind)
    outs_done()


def on_device(n, parts, rhs, lower_tiles, lower_block_columns, upper_tiles, upper_cols, diag_inverse):
    rhs = rhs[:, :, 0]
    lower = lower_tiles[:, :, 0]
    upper = upper_tiles[:, :, 0]
    inverse = diag_inverse[:, :, 0]
    levels, rows, sides, block = rhs.shape
    slots = lower.shape[2]
    owners = 2 * parts
    share = rows // owners
    half = jnp.bfloat16
    dma = pltpu.SemaphoreType.DMA
    any_space = pl.BlockSpec(memory_space=pl.ANY)
    tiles = pltpu.VMEM((levels, 2, share, slots, block, block), half)
    own = pltpu.VMEM((levels, share, owners, sides, block), half)
    result = pl.pallas_call(
        functools.partial(sweep_kernel, n, parts),
        out_shape=jax.ShapeDtypeStruct(rhs.shape, half),
        in_specs=[pl.BlockSpec(memory_space=pltpu.HBM)] * 6,
        out_specs=any_space,
        scratch_shapes=[
            pltpu.SMEM((2, 2, levels, slots, 1, rows), jnp.int32),
            pltpu.VMEM(rhs.shape, rhs.dtype),
            pltpu.VMEM(rhs.shape, half),
            tiles,
            tiles,
            pltpu.VMEM((levels, 2, share, block, block), half),
            pltpu.VMEM((share, 2, 3, block, block), half),
            pltpu.VMEM((share, 2, parts, sides, block), jnp.float32),
            own,
            own,
            pltpu.VMEM((2, levels, share, parts, 2, sides, block), half),
            dma((2,)),
            dma((3,)),
            dma((3, 2)),
            dma((3,)),
            dma((3, levels)),
            dma((1,)),
            dma((levels,)),
            dma((1,)),
            dma((2,)),
            dma((2, share, parts)),
            dma((3,)),
        ],
        compiler_params=pltpu.CompilerParams(collective_id=0, has_side_effects=True, vmem_limit_bytes=VMEM_LIMIT),
    )(
        lower_block_columns.transpose(0, 3, 2, 1),
        upper_cols.transpose(0, 3, 2, 1),
        rhs,
        lower,
        upper,
        inverse,
    )
    return result[:, :, None]


def solution(mesh):
    return jax.shard_map(
        functools.partial(on_device, mesh.shape["blk"], mesh.shape["rhs"]),
        mesh=mesh,
        in_specs=(
            P(None, None, "blk", "rhs", None),
            P(None, None, "blk", None, None, None),
            P(None, None, "blk", None),
            P(None, None, "blk", None, None, None),
            P(None, None, "blk", None),
            P(None, None, "blk", None, None),
        ),
        out_specs=P(None, None, "blk", "rhs", None),
        check_vma=False,
    )
```

```python
import functools

import jax
import jax.numpy as jnp
from jax import lax
from jax.experimental import pallas as pl
from jax.experimental.pallas import tpu as pltpu
from jax.sharding import PartitionSpec as P

MESH = pl.DeviceIdType.MESH
VMEM_LIMIT = 67043328
AHEAD = 4


def product(x, tile):
    return lax.dot_general(x, tile, (((1,), (1,)), ((), ())), preferred_element_type=jnp.float32)


def sweep_kernel(
    n,
    parts,
    lower_cols,
    upper_cols,
    rhs,
    lower,
    upper,
    inverse,
    out,
    cols,
    rhs_v,
    rhs_b,
    lower_v,
    upper_v,
    inverse_v,
    chosen,
    y,
    x,
    halo,
    rhs_sem,
    load_sem,
    cols_sem,
    tile_send,
    tile_recv,
    side_send,
    side_recv,
    row_send,
    row_recv,
    out_sem,
):
    levels, rows, sides, block = rhs.shape
    slots = lower.shape[2]
    owners = 2 * parts
    share = rows // owners
    last = levels - 1
    me = lax.axis_index("blk")
    part = lax.axis_index("rhs")
    half = lax.rem(me, 2)
    pair = me - half
    partner = pair + 1 - half
    owner = half * parts + part
    mine = owner * share
    others = range(1, owners)

    def other(k):
        return lax.rem(owner + k, owners)

    def device(first, s):
        return {"blk": first + s // parts, "rhs": lax.rem(s, parts)}

    def load_rhs(first, count):
        span = pl.ds(first, count)
        return pltpu.make_async_copy(rhs.at[span], rhs_v.at[span], rhs_sem.at[min(first, 1)])

    def tiles_of(kind):
        return ((lower, lower_v), (upper, upper_v), (inverse, inverse_v))[kind]

    spans = (pl.ds(1, last), pl.ds(0, last), pl.ds(0, levels))

    def load(kind):
        source, target = tiles_of(kind)
        span = spans[kind]
        return pltpu.make_async_copy(
            source.at[span, pl.ds(mine, share)], target.at[span, half], load_sem.at[kind]
        )

    def load_cols(kind):
        return pltpu.make_async_copy((lower_cols, upper_cols)[kind], cols.at[half, kind], cols_sem.at[0, kind])

    def remote(source, target, send_sem, recv_sem, device_id):
        return pltpu.make_async_remote_copy(
            src_ref=source,
            dst_ref=target,
            send_sem=send_sem,
            recv_sem=recv_sem,
            device_id=device_id,
            device_id_type=MESH,
        )

    def give_cols(kind):
        return remote(
            (lower_cols, upper_cols)[kind],
            cols.at[half, kind],
            cols_sem.at[1, kind],
            cols_sem.at[2, kind],
            {"blk": partner},
        )

    def give_tiles(kind, level):
        source, target = tiles_of(kind)
        theirs = ((1 - half) * parts + part) * share
        return remote(
            source.at[level, pl.ds(theirs, share)],
            target.at[level, half],
            tile_send.at[kind],
            tile_recv.at[kind, level],
            {"blk": partner},
        )

    def tiles_given(kind):
        source, target = tiles_of(kind)
        span = spans[kind]
        remote(
            source.at[span, pl.ds(0, share)], target.at[span, half], tile_send.at[kind], tile_recv.at[kind, 0], {"blk": partner}
        ).wait_send()

    def give_sides(level, k):
        s = other(k)
        return remote(
            rhs_b.at[level, pl.ds(s * share, share)],
            y.at[level, :, owner],
            side_send.at[0],
            side_recv.at[level],
            device(pair, s),
        )

    def sides_given():
        whole = rhs_b.at[:, pl.ds(0, rows - share)]
        remote(whole, whole, side_send.at[0], side_recv.at[0], {"blk": partner}).wait_send()

    def take_sides(level):
        whole = y.at[level, :, pl.ds(0, owners - 1)]
        remote(whole, whole, side_send.at[0], side_recv.at[level], {"blk": partner}).wait_recv()

    def turn_of(sweep, level):
        return lax.rem(level if sweep == 0 else 2 * last - level, 2)

    def give_row(own, sweep, level, i, j, way):
        return remote(
            own.at[level, i, way * parts + j],
            halo.at[sweep, level, i, j, way],
            row_send.at[sweep],
            row_recv.at[turn_of(sweep, level), i, j],
            {"blk": lax.rem(me + 4 * way - 2 + n, n)},
        )

    def take_rows(sweep, level, i, j):
        whole = halo.at[sweep, level, i, j]
        remote(
            whole, whole, row_send.at[sweep], row_recv.at[turn_of(sweep, level), i, j], {"blk": partner}
        ).wait_recv()

    def rows_given(own, sweep):
        whole = own.at[pl.ds(sweep, last)]
        remote(whole, whole, row_send.at[sweep], row_recv.at[0, 0, 0], {"blk": partner}).wait_send()

    def give_out(level, i, s):
        return remote(
            x.at[level, i, s],
            out.at[level, mine + i],
            out_sem.at[0],
            out_sem.at[1],
            device(pair, s),
        )

    def keep_out(level, i):
        return pltpu.make_async_copy(x.at[level, i, owner], out.at[level, mine + i], out_sem.at[2])

    def leave_piece(level, i, j):
        for s in (j, parts + j):

            @pl.when(owner != s)
            def _():
                give_out(level, i, s).start()

            @pl.when(owner == s)
            def _():
                keep_out(level, i).start()

    def outs_done():
        sent = x.at[:, :, pl.ds(0, owners - 1)]
        kept = x.at[:, :, owner]
        got = out.at[:, pl.ds(0, rows - share)]
        pltpu.make_async_copy(kept, out.at[:, pl.ds(mine, share)], out_sem.at[2]).wait()
        remote(sent, sent, out_sem.at[0], out_sem.at[1], {"blk": partner}).wait_send()
        remote(got, got, out_sem.at[0], out_sem.at[1], {"blk": partner}).wait_recv()

    def each(first, end, action):
        def step(level, carry):
            action(level)
            return carry

        lax.fori_loop(first, end, step, 0)

    load_rhs(0, 1).start()
    barrier = pltpu.get_barrier_semaphore()

    def greet(first, s):
        pl.semaphore_signal(barrier, inc=1, device_id=device(first, s), device_id_type=MESH)

    for way in range(2):
        pl.semaphore_signal(
            barrier, inc=1, device_id={"blk": lax.rem(me + 4 * way - 2 + n, n)}, device_id_type=MESH
        )
    for k in others:
        greet(pair, other(k))
    load_rhs(1, last).start()
    for kind in range(2):
        load_cols(kind).start()
    for kind in range(3):
        load(kind).start()

    def narrow(level):
        rhs_b[level] = rhs_v[level].astype(jnp.bfloat16)
        for i in range(share):
            y[level, i, owner] = rhs_v[level, mine + i].astype(jnp.bfloat16)

    load_rhs(0, 1).wait()
    narrow(0)
    pl.semaphore_wait(barrier, owners + 1)
    for k in others:
        give_sides(0, k).start()
    give_cols(0).start()
    give_cols(1).start()

    def forward_item(level):
        for k in others:
            give_sides(level, k).start()
        give_tiles(0, level).start()

    def backward_item(level):
        @pl.when(level < last)
        def _():
            give_tiles(1, level).start()

        give_tiles(2, level).start()

    def ahead_forward(level):
        @pl.when(level + AHEAD <= last)
        def _():
            forward_item(level + AHEAD)

        @pl.when(level + AHEAD > last)
        def _():
            backward_item(2 * last + 1 - AHEAD - level)

    def ahead_backward(turn):
        @pl.when(turn + AHEAD - 1 <= last)
        def _():
            backward_item(last - turn - AHEAD + 1)

    def open_item(level):
        narrow(level)
        forward_item(level)

    load_rhs(1, last).wait()
    open_item(1)
    take_sides(0)
    for i in range(share):
        for j in range(parts):
            for way in range(2):
                give_row(y, 0, 0, i, j, way).start()
    each(2, AHEAD + 1, open_item)
    each(AHEAD + 1, levels, narrow)
    for kind in range(2):
        load_cols(kind).wait()
        give_cols(kind).wait_recv()
    for kind in range(3):
        load(kind).wait()

    def choose(sweep, level, source, tiles):
        for i in range(share):
            base = (source * rows + mine + i) * n
            for p in range(2):
                for d in range(3):
                    wanted = base + lax.rem(pair + p + d - 1 + n, n)
                    tile = jnp.zeros((block, block), tiles.dtype)
                    for k in range(slots):
                        found = cols[p, sweep, level, k, 0, mine + i] == wanted
                        tile = lax.select(found, tiles[level, p, i, k], tile)
                    chosen[i, p, d] = tile

    def step(own, sweep, level, source, i, j):
        first = own[source, i, j]
        second = own[source, i, parts + j]
        kept = []
        for p in range(2):
            terms = product(first, chosen[i, p, 1 - p]) + product(second, chosen[i, p, 2 - p])
            kept.append(y[level, i, p * parts + j].astype(jnp.float32) - terms)
        take_rows(sweep, source, i, j)
        low = kept[0] - product(halo[sweep, source, i, j, 1], chosen[i, 0, 0])
        high = kept[1] - product(halo[sweep, source, i, j, 0], chosen[i, 1, 2])
        return low.astype(jnp.bfloat16), high.astype(jnp.bfloat16)

    def arrive_forward(level):
        take_sides(level)
        give_tiles(0, level).wait_recv()

    def forward(level):
        arrive_forward(level)
        choose(0, level, level - 1, lower_v)
        for i in range(share):
            for j in range(parts):
                low, high = step(y, 0, level, level - 1, i, j)
                y[level, i, j] = low
                y[level, i, parts + j] = high
                for way in range(2):
                    give_row(y, 0, level, i, j, way).start()
        ahead_forward(level)

    each(1, last, forward)

    def solve(level, i, j, low, high):
        x[level, i, j] = product(low, inverse_v[level, 0, i]).astype(jnp.bfloat16)
        x[level, i, parts + j] = product(high, inverse_v[level, 1, i]).astype(jnp.bfloat16)

    arrive_forward(last)
    give_tiles(2, last).wait_recv()
    choose(0, last, last - 1, lower_v)
    for i in range(share):
        for j in range(parts):
            low, high = step(y, 0, last, last - 1, i, j)
            solve(last, i, j, low, high)
            for way in range(2):
                give_row(x, 1, last, i, j, way).start()
            leave_piece(last, i, j)
    ahead_forward(last)

    def backward(turn):
        level = last - turn
        give_tiles(1, level).wait_recv()
        give_tiles(2, level).wait_recv()
        choose(1, level, level + 1, upper_v)
        for i in range(share):
            for j in range(parts):
                low, high = step(x, 1, level, level + 1, i, j)
                solve(level, i, j, low, high)

                @pl.when(level > 0)
                def _():
                    for way in range(2):
                        give_row(x, 1, level, i, j, way).start()

                leave_piece(level, i, j)

        ahead_backward(turn)

    each(1, levels, backward)

    for kind in range(2):
        give_cols(kind).wait_send()
    sides_given()
    rows_given(y, 0)
    rows_given(x, 1)
    for kind in range(3):
        tiles_given(kind)
    outs_done()


def on_device(n, parts, rhs, lower_tiles, lower_block_columns, upper_tiles, upper_cols, diag_inverse):
    rhs = rhs[:, :, 0]
    lower = lower_tiles[:, :, 0]
    upper = upper_tiles[:, :, 0]
    inverse = diag_inverse[:, :, 0]
    levels, rows, sides, block = rhs.shape
    slots = lower.shape[2]
    owners = 2 * parts
    share = rows // owners
    half = jnp.bfloat16
    dma = pltpu.SemaphoreType.DMA
    any_space = pl.BlockSpec(memory_space=pl.ANY)
    tiles = pltpu.VMEM((levels, 2, share, slots, block, block), half)
    own = pltpu.VMEM((levels, share, owners, sides, block), half)
    result = pl.pallas_call(
        functools.partial(sweep_kernel, n, parts),
        out_shape=jax.ShapeDtypeStruct(rhs.shape, half),
        in_specs=[pl.BlockSpec(memory_space=pltpu.HBM)] * 6,
        out_specs=any_space,
        scratch_shapes=[
            pltpu.SMEM((2, 2, levels, slots, 1, rows), jnp.int32),
            pltpu.VMEM(rhs.shape, rhs.dtype),
            pltpu.VMEM(rhs.shape, half),
            tiles,
            tiles,
            pltpu.VMEM((levels, 2, share, block, block), half),
            pltpu.VMEM((share, 2, 3, block, block), half),
            own,
            own,
            pltpu.VMEM((2, levels, share, parts, 2, sides, block), half),
            dma((2,)),
            dma((3,)),
            dma((3, 2)),
            dma((3,)),
            dma((3, levels)),
            dma((1,)),
            dma((levels,)),
            dma((2,)),
            dma((2, share, parts)),
            dma((3,)),
        ],
        compiler_params=pltpu.CompilerParams(collective_id=0, has_side_effects=True, vmem_limit_bytes=VMEM_LIMIT),
    )(
        lower_block_columns.transpose(0, 3, 2, 1),
        upper_cols.transpose(0, 3, 2, 1),
        rhs,
        lower,
        upper,
        inverse,
    )
    return result[:, :, None]


def solution(mesh):
    return jax.shard_map(
        functools.partial(on_device, mesh.shape["blk"], mesh.shape["rhs"]),
        mesh=mesh,
        in_specs=(
            P(None, None, "blk", "rhs", None),
            P(None, None, "blk", None, None, None),
            P(None, None, "blk", None),
            P(None, None, "blk", None, None, None),
            P(None, None, "blk", None),
            P(None, None, "blk", None, None),
        ),
        out_specs=P(None, None, "blk", "rhs", None),
        check_vma=False,
    )
```

```python
import functools

import jax
import jax.numpy as jnp
from jax import lax
from jax.experimental import pallas as pl
from jax.experimental.pallas import tpu as pltpu
from jax.sharding import PartitionSpec as P

MESH = pl.DeviceIdType.MESH
VMEM_LIMIT = 67043328
AHEAD = 4
SPLIT = 2


def product(x, tile):
    return lax.dot_general(x, tile, (((1,), (1,)), ((), ())), preferred_element_type=jnp.float32)


def sweep_kernel(
    n,
    parts,
    lower_cols,
    upper_cols,
    rhs,
    lower,
    upper,
    inverse,
    out,
    cols,
    rhs_v,
    rhs_b,
    lower_v,
    upper_v,
    inverse_v,
    chosen,
    y,
    x,
    halo,
    rhs_sem,
    load_sem,
    cols_sem,
    tile_send,
    tile_recv,
    side_send,
    side_recv,
    row_send,
    row_recv,
    out_sem,
):
    levels, rows, sides, block = rhs.shape
    slots = lower.shape[2]
    owners = 2 * parts
    share = rows // owners
    last = levels - 1
    me = lax.axis_index("blk")
    part = lax.axis_index("rhs")
    half = lax.rem(me, 2)
    pair = me - half
    partner = pair + 1 - half
    owner = half * parts + part
    mine = owner * share
    others = range(1, owners)
    part_size = sides // SPLIT
    pieces = [(j, pl.ds(u * part_size, part_size)) for j in range(parts) for u in range(SPLIT)]

    def ready(j, span):
        return j * SPLIT + span.start // part_size

    def other(k):
        return lax.rem(owner + k, owners)

    def device(first, s):
        return {"blk": first + s // parts, "rhs": lax.rem(s, parts)}

    def load_rhs(first, count):
        span = pl.ds(first, count)
        return pltpu.make_async_copy(rhs.at[span], rhs_v.at[span], rhs_sem.at[min(first, 1)])

    def tiles_of(kind):
        return ((lower, lower_v), (upper, upper_v), (inverse, inverse_v))[kind]

    spans = (pl.ds(1, last), pl.ds(0, last), pl.ds(0, levels))

    def load(kind):
        source, target = tiles_of(kind)
        span = spans[kind]
        return pltpu.make_async_copy(
            source.at[span, pl.ds(mine, share)], target.at[span, half], load_sem.at[kind]
        )

    def load_cols(kind):
        return pltpu.make_async_copy((lower_cols, upper_cols)[kind], cols.at[half, kind], cols_sem.at[0, kind])

    def remote(source, target, send_sem, recv_sem, device_id):
        return pltpu.make_async_remote_copy(
            src_ref=source,
            dst_ref=target,
            send_sem=send_sem,
            recv_sem=recv_sem,
            device_id=device_id,
            device_id_type=MESH,
        )

    def give_cols(kind):
        return remote(
            (lower_cols, upper_cols)[kind],
            cols.at[half, kind],
            cols_sem.at[1, kind],
            cols_sem.at[2, kind],
            {"blk": partner},
        )

    def give_tiles(kind, level):
        source, target = tiles_of(kind)
        theirs = ((1 - half) * parts + part) * share
        return remote(
            source.at[level, pl.ds(theirs, share)],
            target.at[level, half],
            tile_send.at[kind],
            tile_recv.at[kind, level],
            {"blk": partner},
        )

    def tiles_given(kind):
        source, target = tiles_of(kind)
        span = spans[kind]
        remote(
            source.at[span, pl.ds(0, share)], target.at[span, half], tile_send.at[kind], tile_recv.at[kind, 0], {"blk": partner}
        ).wait_send()

    def give_sides(level, k):
        s = other(k)
        return remote(
            rhs_b.at[level, pl.ds(s * share, share)],
            y.at[level, :, owner],
            side_send.at[0],
            side_recv.at[level],
            device(pair, s),
        )

    def sides_given():
        whole = rhs_b.at[:, pl.ds(0, rows - share)]
        remote(whole, whole, side_send.at[0], side_recv.at[0], {"blk": partner}).wait_send()

    def take_sides(level):
        whole = y.at[level, :, pl.ds(0, owners - 1)]
        remote(whole, whole, side_send.at[0], side_recv.at[level], {"blk": partner}).wait_recv()

    def turn_of(sweep, level):
        return lax.rem(level if sweep == 0 else 2 * last - level, 2)

    def give_row(own, sweep, level, i, j, span, way):
        return remote(
            own.at[level, i, way * parts + j, span],
            halo.at[sweep, level, i, j, way, span],
            row_send.at[sweep],
            row_recv.at[turn_of(sweep, level), i, ready(j, span)],
            {"blk": lax.rem(me + 4 * way - 2 + n, n)},
        )

    def take_rows(sweep, level, i, j, span):
        whole = halo.at[sweep, level, i, j, :, span]
        remote(
            whole, whole, row_send.at[sweep], row_recv.at[turn_of(sweep, level), i, ready(j, span)], {"blk": partner}
        ).wait_recv()

    def rows_given(own, sweep):
        whole = own.at[pl.ds(sweep, last)]
        remote(whole, whole, row_send.at[sweep], row_recv.at[0, 0, 0], {"blk": partner}).wait_send()

    def give_out(level, i, s):
        return remote(
            x.at[level, i, s],
            out.at[level, mine + i],
            out_sem.at[0],
            out_sem.at[1],
            device(pair, s),
        )

    def keep_out(level, i):
        return pltpu.make_async_copy(x.at[level, i, owner], out.at[level, mine + i], out_sem.at[2])

    def leave_piece(level, i, j):
        for s in (j, parts + j):

            @pl.when(owner != s)
            def _():
                give_out(level, i, s).start()

            @pl.when(owner == s)
            def _():
                keep_out(level, i).start()

    def outs_done():
        sent = x.at[:, :, pl.ds(0, owners - 1)]
        kept = x.at[:, :, owner]
        got = out.at[:, pl.ds(0, rows - share)]
        pltpu.make_async_copy(kept, out.at[:, pl.ds(mine, share)], out_sem.at[2]).wait()
        remote(sent, sent, out_sem.at[0], out_sem.at[1], {"blk": partner}).wait_send()
        remote(got, got, out_sem.at[0], out_sem.at[1], {"blk": partner}).wait_recv()

    def each(first, end, action):
        def step(level, carry):
            action(level)
            return carry

        lax.fori_loop(first, end, step, 0)

    load_rhs(0, 1).start()
    barrier = pltpu.get_barrier_semaphore()

    def greet(first, s):
        pl.semaphore_signal(barrier, inc=1, device_id=device(first, s), device_id_type=MESH)

    for way in range(2):
        pl.semaphore_signal(
            barrier, inc=1, device_id={"blk": lax.rem(me + 4 * way - 2 + n, n)}, device_id_type=MESH
        )
    for k in others:
        greet(pair, other(k))
    load_rhs(1, last).start()
    for kind in range(2):
        load_cols(kind).start()
    for kind in range(3):
        load(kind).start()

    def narrow(level):
        rhs_b[level] = rhs_v[level].astype(jnp.bfloat16)
        for i in range(share):
            y[level, i, owner] = rhs_v[level, mine + i].astype(jnp.bfloat16)

    load_rhs(0, 1).wait()
    narrow(0)
    pl.semaphore_wait(barrier, owners + 1)
    for k in others:
        give_sides(0, k).start()
    give_cols(0).start()
    give_cols(1).start()

    def forward_item(level):
        for k in others:
            give_sides(level, k).start()
        give_tiles(0, level).start()

    def backward_item(level):
        @pl.when(level < last)
        def _():
            give_tiles(1, level).start()

        give_tiles(2, level).start()

    def ahead_forward(level):
        @pl.when(level + AHEAD <= last)
        def _():
            forward_item(level + AHEAD)

        @pl.when(level + AHEAD > last)
        def _():
            backward_item(2 * last + 1 - AHEAD - level)

    def ahead_backward(turn):
        @pl.when(turn + AHEAD - 1 <= last)
        def _():
            backward_item(last - turn - AHEAD + 1)

    def open_item(level):
        narrow(level)
        forward_item(level)

    load_rhs(1, last).wait()
    open_item(1)
    take_sides(0)
    for i in range(share):
        for j, span in pieces:
            for way in range(2):
                give_row(y, 0, 0, i, j, span, way).start()
    each(2, AHEAD + 1, open_item)
    each(AHEAD + 1, levels, narrow)
    for kind in range(2):
        load_cols(kind).wait()
        give_cols(kind).wait_recv()
    for kind in range(3):
        load(kind).wait()

    def choose(sweep, level, source, tiles):
        for i in range(share):
            base = (source * rows + mine + i) * n
            for p in range(2):
                for d in range(3):
                    wanted = base + lax.rem(pair + p + d - 1 + n, n)
                    tile = jnp.zeros((block, block), tiles.dtype)
                    for k in range(slots):
                        found = cols[p, sweep, level, k, 0, mine + i] == wanted
                        tile = lax.select(found, tiles[level, p, i, k], tile)
                    chosen[i, p, d] = tile

    def step(own, sweep, level, source, i, j, span):
        first = own[source, i, j, span]
        second = own[source, i, parts + j, span]
        kept = []
        for p in range(2):
            terms = product(first, chosen[i, p, 1 - p]) + product(second, chosen[i, p, 2 - p])
            kept.append(y[level, i, p * parts + j, span].astype(jnp.float32) - terms)
        if sweep == 1:
            kept = [product(kept[p].astype(jnp.bfloat16), inverse_v[level, p, i]) for p in range(2)]
        take_rows(sweep, source, i, j, span)
        low = kept[0] - product(halo[sweep, source, i, j, 1, span], chosen[i, 0, 0])
        high = kept[1] - product(halo[sweep, source, i, j, 0, span], chosen[i, 1, 2])
        return low.astype(jnp.bfloat16), high.astype(jnp.bfloat16)

    def join(level):
        for i in range(share):
            for p in range(2):
                both = lax.dot_general(
                    inverse_v[level, p, i],
                    chosen[i, p, 2 * p],
                    (((1,), (0,)), ((), ())),
                    preferred_element_type=jnp.float32,
                )
                chosen[i, p, 2 * p] = both.astype(jnp.bfloat16)

    def arrive_forward(level):
        take_sides(level)
        give_tiles(0, level).wait_recv()

    def forward(level):
        arrive_forward(level)
        choose(0, level, level - 1, lower_v)
        for i in range(share):
            for j, span in pieces:
                low, high = step(y, 0, level, level - 1, i, j, span)
                y[level, i, j, span] = low
                y[level, i, parts + j, span] = high
                for way in range(2):
                    give_row(y, 0, level, i, j, span, way).start()
        ahead_forward(level)

    each(1, last, forward)

    def solve(level, i, j, span, low, high):
        x[level, i, j, span] = product(low, inverse_v[level, 0, i]).astype(jnp.bfloat16)
        x[level, i, parts + j, span] = product(high, inverse_v[level, 1, i]).astype(jnp.bfloat16)

    arrive_forward(last)
    give_tiles(2, last).wait_recv()
    choose(0, last, last - 1, lower_v)
    for i in range(share):
        for j, span in pieces:
            low, high = step(y, 0, last, last - 1, i, j, span)
            solve(last, i, j, span, low, high)
            for way in range(2):
                give_row(x, 1, last, i, j, span, way).start()
            if span.start + part_size == sides:
                leave_piece(last, i, j)
    ahead_forward(last)

    def backward(turn):
        level = last - turn
        give_tiles(1, level).wait_recv()
        give_tiles(2, level).wait_recv()
        choose(1, level, level + 1, upper_v)
        join(level)
        for i in range(share):
            for j, span in pieces:
                low, high = step(x, 1, level, level + 1, i, j, span)
                x[level, i, j, span] = low
                x[level, i, parts + j, span] = high

                @pl.when(level > 0)
                def _():
                    for way in range(2):
                        give_row(x, 1, level, i, j, span, way).start()

                if span.start + part_size == sides:
                    leave_piece(level, i, j)

        ahead_backward(turn)

    each(1, levels, backward)

    for kind in range(2):
        give_cols(kind).wait_send()
    sides_given()
    rows_given(y, 0)
    rows_given(x, 1)
    for kind in range(3):
        tiles_given(kind)
    outs_done()


def on_device(n, parts, rhs, lower_tiles, lower_block_columns, upper_tiles, upper_cols, diag_inverse):
    rhs = rhs[:, :, 0]
    lower = lower_tiles[:, :, 0]
    upper = upper_tiles[:, :, 0]
    inverse = diag_inverse[:, :, 0]
    levels, rows, sides, block = rhs.shape
    slots = lower.shape[2]
    owners = 2 * parts
    share = rows // owners
    half = jnp.bfloat16
    dma = pltpu.SemaphoreType.DMA
    any_space = pl.BlockSpec(memory_space=pl.ANY)
    tiles = pltpu.VMEM((levels, 2, share, slots, block, block), half)
    own = pltpu.VMEM((levels, share, owners, sides, block), half)
    result = pl.pallas_call(
        functools.partial(sweep_kernel, n, parts),
        out_shape=jax.ShapeDtypeStruct(rhs.shape, half),
        in_specs=[pl.BlockSpec(memory_space=pltpu.HBM)] * 6,
        out_specs=any_space,
        scratch_shapes=[
            pltpu.SMEM((2, 2, levels, slots, 1, rows), jnp.int32),
            pltpu.VMEM(rhs.shape, rhs.dtype),
            pltpu.VMEM(rhs.shape, half),
            tiles,
            tiles,
            pltpu.VMEM((levels, 2, share, block, block), half),
            pltpu.VMEM((share, 2, 3, block, block), half),
            own,
            own,
            pltpu.VMEM((2, levels, share, parts, 2, sides, block), half),
            dma((2,)),
            dma((3,)),
            dma((3, 2)),
            dma((3,)),
            dma((3, levels)),
            dma((1,)),
            dma((levels,)),
            dma((2,)),
            dma((2, share, parts * SPLIT)),
            dma((3,)),
        ],
        compiler_params=pltpu.CompilerParams(collective_id=0, has_side_effects=True, vmem_limit_bytes=VMEM_LIMIT),
    )(
        lower_block_columns.transpose(0, 3, 2, 1),
        upper_cols.transpose(0, 3, 2, 1),
        rhs,
        lower,
        upper,
        inverse,
    )
    return result[:, :, None]


def solution(mesh):
    return jax.shard_map(
        functools.partial(on_device, mesh.shape["blk"], mesh.shape["rhs"]),
        mesh=mesh,
        in_specs=(
            P(None, None, "blk", "rhs", None),
            P(None, None, "blk", None, None, None),
            P(None, None, "blk", None),
            P(None, None, "blk", None, None, None),
            P(None, None, "blk", None),
            P(None, None, "blk", None, None),
        ),
        out_specs=P(None, None, "blk", "rhs", None),
        check_vma=False,
    )
```

```python
import functools

import jax
import jax.numpy as jnp
from jax import lax
from jax.experimental import pallas as pl
from jax.experimental.pallas import tpu as pltpu
from jax.sharding import PartitionSpec as P

MESH = pl.DeviceIdType.MESH
VMEM_LIMIT = 67043328
AHEAD = 4
SPLIT = 2


def product(x, tile):
    return lax.dot_general(x, tile, (((1,), (1,)), ((), ())), preferred_element_type=jnp.float32)


def sweep_kernel(
    n,
    parts,
    lower_cols,
    upper_cols,
    rhs,
    lower,
    upper,
    inverse,
    out,
    cols,
    rhs_v,
    rhs_b,
    lower_v,
    upper_v,
    inverse_v,
    chosen,
    y,
    x,
    halo,
    rhs_sem,
    load_sem,
    cols_sem,
    tile_send,
    tile_recv,
    side_send,
    side_recv,
    row_send,
    row_recv,
    out_sem,
):
    levels, rows, sides, block = rhs.shape
    slots = lower.shape[2]
    owners = 2 * parts
    share = rows // owners
    last = levels - 1
    me = lax.axis_index("blk")
    part = lax.axis_index("rhs")
    half = lax.rem(me, 2)
    pair = me - half
    partner = pair + 1 - half
    owner = half * parts + part
    mine = owner * share
    others = range(1, owners)
    part_size = sides // SPLIT
    pieces = [(j, pl.ds(u * part_size, part_size)) for j in range(parts) for u in range(SPLIT)]

    def ready(j, span):
        return j * SPLIT + span.start // part_size

    def other(k):
        return lax.rem(owner + k, owners)

    def device(first, s):
        return {"blk": first + s // parts, "rhs": lax.rem(s, parts)}

    def load_rhs(first, count):
        span = pl.ds(first, count)
        return pltpu.make_async_copy(rhs.at[span], rhs_v.at[span], rhs_sem.at[min(first, 1)])

    def tiles_of(kind):
        return ((lower, lower_v), (upper, upper_v), (inverse, inverse_v))[kind]

    spans = (pl.ds(1, last), pl.ds(0, last), pl.ds(0, levels))

    def load(kind):
        source, target = tiles_of(kind)
        span = spans[kind]
        return pltpu.make_async_copy(
            source.at[span, pl.ds(mine, share)], target.at[span, half], load_sem.at[kind]
        )

    def load_cols(kind):
        return pltpu.make_async_copy((lower_cols, upper_cols)[kind], cols.at[half, kind], cols_sem.at[0, kind])

    def remote(source, target, send_sem, recv_sem, device_id):
        return pltpu.make_async_remote_copy(
            src_ref=source,
            dst_ref=target,
            send_sem=send_sem,
            recv_sem=recv_sem,
            device_id=device_id,
            device_id_type=MESH,
        )

    def give_cols(kind):
        return remote(
            (lower_cols, upper_cols)[kind],
            cols.at[half, kind],
            cols_sem.at[1, kind],
            cols_sem.at[2, kind],
            {"blk": partner},
        )

    def give_tiles(kind, level):
        source, target = tiles_of(kind)
        theirs = ((1 - half) * parts + part) * share
        return remote(
            source.at[level, pl.ds(theirs, share)],
            target.at[level, half],
            tile_send.at[kind],
            tile_recv.at[kind, level],
            {"blk": partner},
        )

    def tiles_given(kind):
        source, target = tiles_of(kind)
        span = spans[kind]
        remote(
            source.at[span, pl.ds(0, share)], target.at[span, half], tile_send.at[kind], tile_recv.at[kind, 0], {"blk": partner}
        ).wait_send()

    def give_sides(level, k):
        s = other(k)
        return remote(
            rhs_b.at[level, pl.ds(s * share, share)],
            y.at[level, :, owner],
            side_send.at[0],
            side_recv.at[level],
            device(pair, s),
        )

    def sides_given():
        whole = rhs_b.at[:, pl.ds(0, rows - share)]
        remote(whole, whole, side_send.at[0], side_recv.at[0], {"blk": partner}).wait_send()

    def take_sides(level):
        whole = y.at[level, :, pl.ds(0, owners - 1)]
        remote(whole, whole, side_send.at[0], side_recv.at[level], {"blk": partner}).wait_recv()

    def turn_of(sweep, level):
        return lax.rem(level if sweep == 0 else 2 * last - level, 2)

    def give_row(own, sweep, level, i, j, span, way):
        return remote(
            own.at[level, i, way * parts + j, span],
            halo.at[sweep, level, i, j, way, span],
            row_send.at[sweep],
            row_recv.at[turn_of(sweep, level), i, ready(j, span)],
            {"blk": lax.rem(me + 4 * way - 2 + n, n)},
        )

    def take_rows(sweep, level, i, j, span):
        whole = halo.at[sweep, level, i, j, :, span]
        remote(
            whole, whole, row_send.at[sweep], row_recv.at[turn_of(sweep, level), i, ready(j, span)], {"blk": partner}
        ).wait_recv()

    def rows_given(own, sweep):
        whole = own.at[pl.ds(sweep, last)]
        remote(whole, whole, row_send.at[sweep], row_recv.at[0, 0, 0], {"blk": partner}).wait_send()

    def give_out(level, i, s):
        return remote(
            x.at[level, i, s],
            out.at[level, mine + i],
            out_sem.at[0],
            out_sem.at[1],
            device(pair, s),
        )

    def keep_out(level, i):
        return pltpu.make_async_copy(x.at[level, i, owner], out.at[level, mine + i], out_sem.at[2])

    def leave_piece(level, i, j):
        for s in (j, parts + j):

            @pl.when(owner != s)
            def _():
                give_out(level, i, s).start()

            @pl.when(owner == s)
            def _():
                keep_out(level, i).start()

    def outs_done():
        sent = x.at[:, :, pl.ds(0, owners - 1)]
        kept = x.at[:, :, owner]
        got = out.at[:, pl.ds(0, rows - share)]
        pltpu.make_async_copy(kept, out.at[:, pl.ds(mine, share)], out_sem.at[2]).wait()
        remote(sent, sent, out_sem.at[0], out_sem.at[1], {"blk": partner}).wait_send()
        remote(got, got, out_sem.at[0], out_sem.at[1], {"blk": partner}).wait_recv()

    def each(first, end, action):
        def step(level, carry):
            action(level)
            return carry

        lax.fori_loop(first, end, step, 0)

    load_rhs(0, 1).start()
    barrier = pltpu.get_barrier_semaphore()

    def greet(first, s):
        pl.semaphore_signal(barrier, inc=1, device_id=device(first, s), device_id_type=MESH)

    for way in range(2):
        pl.semaphore_signal(
            barrier, inc=1, device_id={"blk": lax.rem(me + 4 * way - 2 + n, n)}, device_id_type=MESH
        )
    for k in others:
        greet(pair, other(k))
    load_rhs(1, last).start()
    for kind in range(2):
        load_cols(kind).start()
    for kind in range(3):
        load(kind).start()

    def narrow(level):
        rhs_b[level] = rhs_v[level].astype(jnp.bfloat16)
        for i in range(share):
            y[level, i, owner] = rhs_v[level, mine + i].astype(jnp.bfloat16)

    load_rhs(0, 1).wait()
    narrow(0)
    pl.semaphore_wait(barrier, owners + 1)
    for k in others:
        give_sides(0, k).start()
    give_cols(0).start()
    give_cols(1).start()

    def forward_item(level):
        give_tiles(0, level).start()
        for k in others:
            give_sides(level, k).start()

    def backward_item(level):
        @pl.when(level < last)
        def _():
            give_tiles(1, level).start()

        give_tiles(2, level).start()

    def ahead_forward(level):
        @pl.when(level + AHEAD <= last)
        def _():
            forward_item(level + AHEAD)

        @pl.when(level + AHEAD > last)
        def _():
            backward_item(2 * last + 1 - AHEAD - level)

    def ahead_backward(turn):
        @pl.when(turn + AHEAD - 1 <= last)
        def _():
            backward_item(last - turn - AHEAD + 1)

    def open_item(level):
        narrow(level)
        forward_item(level)

    load_rhs(1, last).wait()
    open_item(1)
    take_sides(0)
    for i in range(share):
        for j, span in pieces:
            for way in range(2):
                give_row(y, 0, 0, i, j, span, way).start()
    each(2, AHEAD + 1, open_item)
    each(AHEAD + 1, levels, narrow)
    for kind in range(2):
        load_cols(kind).wait()
        give_cols(kind).wait_recv()
    for kind in range(3):
        load(kind).wait()

    def choose(sweep, level, source, tiles):
        for i in range(share):
            base = (source * rows + mine + i) * n
            for p in range(2):
                for d in range(3):
                    wanted = base + lax.rem(pair + p + d - 1 + n, n)
                    tile = jnp.zeros((block, block), tiles.dtype)
                    for k in range(slots):
                        found = cols[p, sweep, level, k, 0, mine + i] == wanted
                        tile = lax.select(found, tiles[level, p, i, k], tile)
                    chosen[i, p, d] = tile

    def step(own, sweep, level, source, i, j, span):
        first = own[source, i, j, span]
        second = own[source, i, parts + j, span]
        kept = []
        for p in range(2):
            terms = product(first, chosen[i, p, 1 - p]) + product(second, chosen[i, p, 2 - p])
            kept.append(y[level, i, p * parts + j, span].astype(jnp.float32) - terms)
        if sweep == 1:
            kept = [product(kept[p].astype(jnp.bfloat16), inverse_v[level, p, i]) for p in range(2)]
        take_rows(sweep, source, i, j, span)
        low = kept[0] - product(halo[sweep, source, i, j, 1, span], chosen[i, 0, 0])
        high = kept[1] - product(halo[sweep, source, i, j, 0, span], chosen[i, 1, 2])
        return low.astype(jnp.bfloat16), high.astype(jnp.bfloat16)

    def join(level):
        for i in range(share):
            for p in range(2):
                both = lax.dot_general(
                    inverse_v[level, p, i],
                    chosen[i, p, 2 * p],
                    (((1,), (0,)), ((), ())),
                    preferred_element_type=jnp.float32,
                )
                chosen[i, p, 2 * p] = both.astype(jnp.bfloat16)

    def arrive_forward(level):
        take_sides(level)
        give_tiles(0, level).wait_recv()

    def forward(level):
        arrive_forward(level)
        choose(0, level, level - 1, lower_v)
        for i in range(share):
            for j, span in pieces:
                low, high = step(y, 0, level, level - 1, i, j, span)
                y[level, i, j, span] = low
                y[level, i, parts + j, span] = high
                for way in range(2):
                    give_row(y, 0, level, i, j, span, way).start()
        ahead_forward(level)

    each(1, last, forward)

    def solve(level, i, j, span, low, high):
        x[level, i, j, span] = product(low, inverse_v[level, 0, i]).astype(jnp.bfloat16)
        x[level, i, parts + j, span] = product(high, inverse_v[level, 1, i]).astype(jnp.bfloat16)

    arrive_forward(last)
    give_tiles(2, last).wait_recv()
    choose(0, last, last - 1, lower_v)
    for i in range(share):
        for j, span in pieces:
            low, high = step(y, 0, last, last - 1, i, j, span)
            solve(last, i, j, span, low, high)
            for way in range(2):
                give_row(x, 1, last, i, j, span, way).start()
            if span.start + part_size == sides:
                leave_piece(last, i, j)
    ahead_forward(last)

    def backward(turn):
        level = last - turn
        give_tiles(1, level).wait_recv()
        give_tiles(2, level).wait_recv()
        choose(1, level, level + 1, upper_v)
        join(level)
        for i in range(share):
            for j, span in pieces:
                low, high = step(x, 1, level, level + 1, i, j, span)
                x[level, i, j, span] = low
                x[level, i, parts + j, span] = high

                @pl.when(level > 0)
                def _():
                    for way in range(2):
                        give_row(x, 1, level, i, j, span, way).start()

                if span.start + part_size == sides:
                    leave_piece(level, i, j)

        ahead_backward(turn)

    each(1, levels, backward)

    for kind in range(2):
        give_cols(kind).wait_send()
    sides_given()
    rows_given(y, 0)
    rows_given(x, 1)
    for kind in range(3):
        tiles_given(kind)
    outs_done()


def on_device(n, parts, rhs, lower_tiles, lower_block_columns, upper_tiles, upper_cols, diag_inverse):
    rhs = rhs[:, :, 0]
    lower = lower_tiles[:, :, 0]
    upper = upper_tiles[:, :, 0]
    inverse = diag_inverse[:, :, 0]
    levels, rows, sides, block = rhs.shape
    slots = lower.shape[2]
    owners = 2 * parts
    share = rows // owners
    half = jnp.bfloat16
    dma = pltpu.SemaphoreType.DMA
    any_space = pl.BlockSpec(memory_space=pl.ANY)
    tiles = pltpu.VMEM((levels, 2, share, slots, block, block), half)
    own = pltpu.VMEM((levels, share, owners, sides, block), half)
    result = pl.pallas_call(
        functools.partial(sweep_kernel, n, parts),
        out_shape=jax.ShapeDtypeStruct(rhs.shape, half),
        in_specs=[pl.BlockSpec(memory_space=pltpu.HBM)] * 6,
        out_specs=any_space,
        scratch_shapes=[
            pltpu.SMEM((2, 2, levels, slots, 1, rows), jnp.int32),
            pltpu.VMEM(rhs.shape, rhs.dtype),
            pltpu.VMEM(rhs.shape, half),
            tiles,
            tiles,
            pltpu.VMEM((levels, 2, share, block, block), half),
            pltpu.VMEM((share, 2, 3, block, block), half),
            own,
            own,
            pltpu.VMEM((2, levels, share, parts, 2, sides, block), half),
            dma((2,)),
            dma((3,)),
            dma((3, 2)),
            dma((3,)),
            dma((3, levels)),
            dma((1,)),
            dma((levels,)),
            dma((2,)),
            dma((2, share, parts * SPLIT)),
            dma((3,)),
        ],
        compiler_params=pltpu.CompilerParams(collective_id=0, has_side_effects=True, vmem_limit_bytes=VMEM_LIMIT),
    )(
        lower_block_columns.transpose(0, 3, 2, 1),
        upper_cols.transpose(0, 3, 2, 1),
        rhs,
        lower,
        upper,
        inverse,
    )
    return result[:, :, None]


def solution(mesh):
    return jax.shard_map(
        functools.partial(on_device, mesh.shape["blk"], mesh.shape["rhs"]),
        mesh=mesh,
        in_specs=(
            P(None, None, "blk", "rhs", None),
            P(None, None, "blk", None, None, None),
            P(None, None, "blk", None),
            P(None, None, "blk", None, None, None),
            P(None, None, "blk", None),
            P(None, None, "blk", None, None),
        ),
        out_specs=P(None, None, "blk", "rhs", None),
        check_vma=False,
    )
```
